32 devices in a mesh: groups: 2 (over y), rows: 4 (over z), zero: 4 (over x, core).
Axes of the slice: x: 2, y: 2, z: 4, core: 2. Of those that a mesh axis runs over, the one named last changes fastest.
Arguments:
- latents: bfloat16 [8, 320, 32, 128], P(('groups', 'zero'), None, 'rows'), parts along dimension 0, may hold values from -40 to 40
- time_shift: float32 [8, 320], P(('groups', 'zero')), parts along dimension 0, may hold values from -4 to 4
- conv_first: bfloat16 [320, 9, 320], P('zero'), may hold values from -0.109375 to 0.109375
- conv_second: bfloat16 [320, 9, 320], P('zero'), may hold values from -0.1875 to 0.1875
- norm_gains: float32 [2, 320], replicated, may hold values from 0.5 to 1.5
- norm_biases: float32 [2, 320], replicated, may hold values from -3 to 3
- grad_output: bfloat16 [8, 320, 32, 128], P(('groups', 'zero'), None, 'rows'), parts along dimension 0, may hold values from -40 to 40
Outputs:
- block_out: bfloat16 [8, 320, 32, 128], P(('groups', 'zero'), None, 'rows'), parts along dimension 0
- grad_input: bfloat16 [8, 320, 32, 128], P(('groups', 'zero'), None, 'rows'), parts along dimension 0
- grad_time: float32 [8, 320], P(('groups', 'zero')), parts along dimension 0
- grad_conv_first: float32 [640, 9, 320], P(('groups', 'zero')), parts along dimension 0
- grad_conv_second: float32 [640, 9, 320], P(('groups', 'zero')), parts along dimension 0
- grad_norms: float32 [8, 320], P('groups'), parts along dimension 0
The draws below stay inside these ranges and needn't reach their ends.
There are 2 independent parts, one for each index of `groups`. The reference program is written for one: setup_inputs(seed, part) draws one part's arguments, and reference() takes and returns one part's arrays. A program takes and returns all parts, laid end to end along the dimension named above; an argument that names none is the same for every part. Nothing has to cross between parts.
All inputs are finite; a program needn't handle non-finite values.
Results may differ from the reference program's by a relative error of at most 0.0056.
Values may be sent and summed in bfloat16 or wider, within the bound.
A program may use at most 128 MiB of HBM per device.

```python
import jax
import jax.numpy as jnp
from jax import lax

C = 320
NORM_GROUPS = 32
W = 128
H = 32
IMAGES = 4


def latent_field(key):
    base_key, row_key, col_key = jax.random.split(key, 3)
    positions = jnp.arange(H, dtype=jnp.float32)
    rising = jnp.exp(jnp.log(3.0) * (positions / max(H - 1, 1) - 0.5))
    row_scale = 10.0 ** (jax.random.uniform(row_key, (H,), jnp.float32) - 0.5)
    col_scale = 10.0 ** (0.5 * jax.random.uniform(col_key, (W,), jnp.float32) - 0.25)
    sampled = jnp.clip(jax.random.normal(base_key, (IMAGES, C, H, W), jnp.float32), -4.0, 4.0)
    result_field = sampled * (rising * row_scale)[:, None] * col_scale[None, :]
    return result_field.astype(jnp.bfloat16)


def draw_latents(key, part):
    return latent_field(jax.random.fold_in(key, 11))


def draw_grad_output(key, part):
    return latent_field(jax.random.fold_in(key, 23))


def shard_levels(rng, dims, pieces, least, high):
    def one(axis_at, shards_of):
        steps = jax.random.uniform(jax.random.fold_in(jax.random.fold_in(rng, 6), axis_at), (shards_of,), jnp.float32, least / len(pieces), high / len(pieces))
        return jnp.repeat(jnp.exp(steps), dims[axis_at] // shards_of).reshape((-1,) + (1,) * (len(dims) - axis_at - 1))

    factor_of = one(*pieces[0])
    for cut in pieces[1:]:
        factor_of = factor_of * one(*cut)
    return factor_of


def normal_values(own_key, shape, spread, bound, shards=(), kind=jnp.bfloat16):
    values = spread * jax.random.normal(own_key, shape, jnp.float32)
    if shards:
        values = values * shard_levels(own_key, shape, shards, -0.22, 0.18)
    return jnp.clip(values, -bound, bound).astype(kind)


def setup_inputs(seed: int = 0, part: int = 0) -> dict:
    key_of = jax.random.split(jax.random.key(seed), 8)
    part_keys = jax.random.split(jax.random.fold_in(key_of[7], part), 8)
    latents = draw_latents(jax.random.fold_in(jax.random.fold_in(key_of[7], part), 71), part)
    time_shift = normal_values(part_keys[1], (IMAGES, C), 1.0, 4.0, ((0, 4),), jnp.float32)
    conv_first = normal_values(key_of[2], (C, 9, C), (9 * C) ** -0.5, 0.109375, ((0, 4),))
    conv_second = normal_values(key_of[3], (C, 9, C), (3 * C) ** -0.5, 0.1875, ((0, 4),))
    norm_gains = jnp.clip(jax.random.uniform(key_of[4], (2, C), jnp.float32, 0.5, 1.5), 0.5, 1.5)
    norm_biases = normal_values(key_of[5], (2, C), 0.5, 3.0, (), jnp.float32)
    grad_output = draw_grad_output(jax.random.fold_in(jax.random.fold_in(key_of[7], part), 71), part)
    return {"latents": latents, "time_shift": time_shift, "conv_first": conv_first, "conv_second": conv_second, "norm_gains": norm_gains, "norm_biases": norm_biases, "grad_output": grad_output}


EPSILON = 1e-05

def shifted_stack(field, flipped):
    padded = jnp.pad(field, ((0, 0), (1, 1), (1, 1)))
    slices = [padded[:, tap_row:tap_row + H, tap_col:tap_col + W] for tap_row in range(3) for tap_col in range(3)]
    if flipped:
        slices = slices[::-1]
    return jnp.stack(slices, axis=0).astype(jnp.float32)

def convolve(field, weights):
    return jnp.einsum('otc,tchw->ohw', weights.astype(jnp.float32), shifted_stack(field, False))

def convolve_back(field, weights):
    return jnp.einsum('otc,tohw->chw', weights.astype(jnp.float32), shifted_stack(field, True))

def weight_grad(cotangent, field):
    return jnp.einsum('ohw,tchw->otc', cotangent.astype(jnp.float32), shifted_stack(field, False))

def group_norm(values):
    grouped = values.reshape(NORM_GROUPS, C // NORM_GROUPS, H, W)
    average = lax.optimization_barrier(jnp.mean(grouped, axis=(1, 2, 3), keepdims=True))
    centered = grouped - average
    variance = lax.optimization_barrier(jnp.mean(centered * centered, axis=(1, 2, 3), keepdims=True))
    scaling = lax.rsqrt(variance + EPSILON)
    return ((centered * scaling).reshape(C, H, W), scaling)

def norm_back(grad_normed, normed, scaling):
    members = C // NORM_GROUPS * H * W
    grouped_grad = grad_normed.reshape(NORM_GROUPS, C // NORM_GROUPS, H, W)
    grouped_norm = normed.reshape(NORM_GROUPS, C // NORM_GROUPS, H, W)
    group_sum = lax.optimization_barrier(jnp.sum(grouped_grad, axis=(1, 2, 3), keepdims=True))
    cross_sum = lax.optimization_barrier(jnp.sum(grouped_grad * grouped_norm, axis=(1, 2, 3), keepdims=True))
    result = scaling * (grouped_grad - group_sum / members - grouped_norm * cross_sum / members)
    return result.reshape(C, H, W)

def silu_slope(pre_values):
    logistic = jax.nn.sigmoid(pre_values)
    return logistic * (1.0 + pre_values * (1.0 - logistic))

def reference(latents, time_shift, conv_first, conv_second, norm_gains, norm_biases, grad_output):
    gain_first = norm_gains[0][:, None, None]
    gain_second = norm_gains[1][:, None, None]
    bias_first = norm_biases[0][:, None, None]
    bias_second = norm_biases[1][:, None, None]

    def one_image(carry, inputs):
        grad_first, grad_second, norm_terms = carry
        latent, shift_row, cotangent = inputs
        normed_first, scale_first = group_norm(latent.astype(jnp.float32))
        pre_first = gain_first * normed_first + bias_first
        act_first = jax.nn.silu(pre_first).astype(jnp.bfloat16)
        hidden = (convolve(act_first, conv_first) + shift_row[:, None, None]).astype(jnp.bfloat16)
        normed_second, scale_second = group_norm(hidden.astype(jnp.float32))
        pre_second = gain_second * normed_second + bias_second
        act_second = jax.nn.silu(pre_second).astype(jnp.bfloat16)
        block = (latent.astype(jnp.float32) + convolve(act_second, conv_second)).astype(jnp.bfloat16)
        grad_second = grad_second + weight_grad(cotangent, act_second)
        back_second = convolve_back(cotangent, conv_second)
        slope_second = back_second * silu_slope(pre_second)
        grad_hidden = norm_back(gain_second * slope_second, normed_second, scale_second)
        time_grad = lax.optimization_barrier(jnp.sum(grad_hidden, axis=(1, 2)))
        hidden_grad = grad_hidden.astype(jnp.bfloat16)
        grad_first = grad_first + weight_grad(hidden_grad, act_first)
        back_first = convolve_back(hidden_grad, conv_first)
        slope_first = back_first * silu_slope(pre_first)
        grad_latent = norm_back(gain_first * slope_first, normed_first, scale_first)
        grad_in = (cotangent.astype(jnp.float32) + grad_latent).astype(jnp.bfloat16)
        local_terms = jnp.stack([lax.optimization_barrier(jnp.sum(slope_first * normed_first, axis=(1, 2))), lax.optimization_barrier(jnp.sum(slope_first, axis=(1, 2))), lax.optimization_barrier(jnp.sum(slope_second * normed_second, axis=(1, 2))), lax.optimization_barrier(jnp.sum(slope_second, axis=(1, 2)))])
        return ((grad_first, grad_second, norm_terms + local_terms), (block, grad_in, time_grad))
    initial = (jnp.zeros((C, 9, C), jnp.float32), jnp.zeros((C, 9, C), jnp.float32), jnp.zeros((4, C), jnp.float32))
    finals, stacked = lax.scan(one_image, initial, (latents, time_shift, grad_output))
    grad_first, grad_second, grad_norms = finals
    block_out, grad_input, grad_time = stacked
    return (block_out, grad_input, grad_time, grad_first, grad_second, grad_norms)
```

```python
import functools

import jax
import jax.numpy as jnp
from jax import lax
from jax.experimental import pallas as pl
from jax.experimental.pallas import tpu as pltpu
from jax.sharding import PartitionSpec as P

NORM_GROUPS = 32
EPSILON = 1e-05
LANES = 128
F32 = jnp.float32
BF16 = jnp.bfloat16
MESH = pl.DeviceIdType.MESH


def block_kernel(
    x, g, pv, w1s, w2s, pool, spread,
    out, gin, small, dw1, dw2,
    act_stack, mid_stack, cot_stack, wfull1, wfull2, wturn,
    normed1, normed2, back, hgrad, cols, stat, halo_out, halo_in,
    part, core_in, core_keep, x_in, z_out, z_in, z_all, tiny, tiny_x,
    send, recv,
):
    channels, cells = x.shape
    height = cells // LANES
    shard = w1s.shape[0]
    rows = lax.axis_size("rows")
    row = lax.axis_index("rows")
    zero = lax.axis_index("zero")
    core = lax.rem(zero, 2)
    mate = zero + 1 - 2 * core
    over = lax.rem(zero + 2, 4)
    over_mate = lax.rem(mate + 2, 4)
    blocks = channels // shard
    members = float(channels // NORM_GROUPS * cells * rows)
    lane = lax.broadcasted_iota(jnp.int32, (shard, LANES), 1)
    wide = lax.broadcasted_iota(jnp.int32, (channels, LANES), 1)
    counter = [0]

    def number():
        counter[0] += 1
        return counter[0] - 1

    pending = []

    def remote(src, dst, target):
        i = number()
        copy = pltpu.make_async_remote_copy(
            src_ref=src, dst_ref=dst, send_sem=send.at[i], recv_sem=recv.at[i],
            device_id=target, device_id_type=MESH,
        )
        return copy

    def go(src, dst, target):
        copy = remote(src, dst, target)
        copy.start()
        pending.append(copy)
        return copy

    def to_rows(src, dst):
        return [go(src, dst, {"rows": lax.rem(row + d, rows)}) for d in range(1, rows)]

    def chunked(body):
        def step(c, _):
            body(pl.multiple_of(c * shard, shard))
            return 0
        lax.fori_loop(0, blocks, step, 0)

    def put(stack, value, start, p, flip):
        left = jnp.where(lane == 0, 0.0, pltpu.roll(value, 1, 1)).astype(BF16)
        right = jnp.where(lane == LANES - 1, 0.0, pltpu.roll(value, LANES - 1, 1)).astype(BF16)
        slabs = (left, value.astype(BF16), right)
        for ty in range(3):
            h = p - 2 + ty if flip else p - ty
            if 0 <= h < height:
                for tx in range(3):
                    tap = 3 * ty + tx
                    stack[pl.ds(start + tap * channels, shard), h * LANES : (h + 1) * LANES] = (
                        slabs[2 - tx if flip else tx]
                    )

    def line(h):
        return slice(h * LANES, (h + 1) * LANES)

    def halo_start(stage, top, bottom):
        down = remote(bottom, halo_in.at[stage, 0], {"rows": lax.rem(row + 1, rows)})
        up = remote(top, halo_in.at[stage, 1], {"rows": lax.rem(row + rows - 1, rows)})

        @pl.when(row < rows - 1)
        def _():
            down.start()

        @pl.when(row > 0)
        def _():
            up.start()

        return down, up

    def halo_finish(stage, pair, stack, flip):
        down, up = pair

        @pl.when(row > 0)
        def _():
            down.wait_recv()
            up.wait_send()

        @pl.when(row < rows - 1)
        def _():
            up.wait_recv()
            down.wait_send()

        @pl.when(row == 0)
        def _():
            halo_in[stage, 0] = jnp.zeros((channels, LANES), BF16)

        @pl.when(row == rows - 1)
        def _():
            halo_in[stage, 1] = jnp.zeros((channels, LANES), BF16)

        def body(start):
            put(stack, halo_in[stage, 0, pl.ds(start, shard), :].astype(F32), start, 0, flip)
            put(stack, halo_in[stage, 1, pl.ds(start, shard), :].astype(F32), start, height + 1, flip)
        chunked(body)

    def lane_sum(value):
        return jnp.sum(value, axis=1, keepdims=True)

    def stat_start(stage, first, second):
        packed = jnp.where(wide == 0, first, jnp.where(wide == 1, second, 0.0))
        stat[stage, row] = jnp.dot(
            pool[...], packed, precision=lax.Precision.HIGHEST, preferred_element_type=F32
        )
        return to_rows(stat.at[stage, row], stat.at[stage, row])

    def stat_finish(stage, copies):
        for copy in copies:
            copy.wait_recv()
        total = stat[stage, 0]
        for i in range(1, rows):
            total = total + stat[stage, i]
        wide_total = jnp.dot(
            spread[...], total, precision=lax.Precision.HIGHEST, preferred_element_type=F32
        ) / members
        return wide_total[:, 0:1], wide_total[:, 1:2]

    def column(i, value):
        cols[i] = jnp.broadcast_to(value, (channels, LANES))

    def moments(stage, copies, at):
        average, square = stat_finish(stage, copies)
        column(at, average)
        column(at + 1, lax.rsqrt(square - average * average + EPSILON))

    barrier = pltpu.get_barrier_semaphore()
    for d in range(1, rows):
        pl.semaphore_signal(
            barrier, inc=1, device_id={"rows": lax.rem(row + d, rows)}, device_id_type=MESH
        )
    for target in (mate, over):
        pl.semaphore_signal(barrier, inc=1, device_id={"zero": target}, device_id_type=MESH)

    SUM_A, SUM_B, SUM_C, SUM_D, SUM_T = 13, 14, 15, 16, 17
    for i in range(5):
        column(8 + i, pv[:, i : i + 1])

    def first_sums(start):
        total = jnp.zeros((shard, LANES), F32)
        square = total
        for h in range(height):
            value = x[pl.ds(start, shard), line(h)].astype(F32)
            total = total + value
            square = square + value * value
        cols[SUM_A, pl.ds(start, shard), :] = total
        cols[SUM_B, pl.ds(start, shard), :] = square
    chunked(first_sums)
    s0, s1 = lane_sum(cols[SUM_A]), lane_sum(cols[SUM_B])

    pl.semaphore_wait(barrier, rows - 1 + 2)
    stat0 = stat_start(0, s0, s1)
    halo_g = halo_start(0, g.at[:, 0:LANES], g.at[:, (height - 1) * LANES : height * LANES])

    def gather_start(own, full):
        near = go(own, full.at[zero], {"zero": mate})
        far = go(own, full.at[zero], {"zero": over})
        return near, far

    def gather_pass(full, far):
        far.wait_recv()
        return go(full.at[over], full.at[over], {"zero": mate})

    gather1 = gather_start(w1s, wfull1)
    gather2 = gather_start(w2s, wfull2)
    wfull1[zero] = w1s[...]
    wfull2[zero] = w2s[...]

    moments(0, stat0, 0)

    def first_act(start):
        at = pl.ds(start, shard)
        for h in range(height):
            normed = (x[at, line(h)].astype(F32) - cols[0, at, :]) * cols[1, at, :]
            normed1[at, line(h)] = normed
            pre = cols[8, at, :] * normed + cols[9, at, :]
            act = (pre / (1.0 + jnp.exp(-pre))).astype(BF16).astype(F32)
            put(act_stack, act, start, h + 1, False)
            if h == 0:
                halo_out[0, 0, at, :] = act.astype(BF16)
            if h == height - 1:
                halo_out[0, 1, at, :] = act.astype(BF16)
    chunked(first_act)
    halo_a = halo_start(1, halo_out.at[0, 0], halo_out.at[0, 1])

    def cot_fill(start):
        for h in range(height):
            put(cot_stack, g[pl.ds(start, shard), line(h)].astype(F32), start, h + 1, True)
    chunked(cot_fill)
    halo_finish(0, halo_g, cot_stack, True)
    pass1 = gather_pass(wfull1, gather1[1])
    halo_finish(1, halo_a, act_stack, False)
    gather1[0].wait_recv()
    pass1.wait_recv()

    TILE = 256

    def tiles(body):
        def step(i, _):
            body(pl.ds(pl.multiple_of(i * TILE, TILE), TILE))
            return 0
        lax.fori_loop(0, cells // TILE, step, 0)

    def conv(full, stack, emit):
        def tile(at):
            weights = full[...].reshape(channels, full.shape[2])
            emit(at, jnp.dot(weights, stack[:, at], preferred_element_type=F32))
        tiles(tile)

    def emit_hidden(at, value):
        shift = cols[12][:, 0:1]
        normed2[:, at] = (value + shift).astype(BF16).astype(F32)
    conv(wfull1, act_stack, emit_hidden)

    def second_sums(start):
        total = jnp.zeros((shard, LANES), F32)
        square = total
        for h in range(height):
            value = normed2[pl.ds(start, shard), line(h)]
            total = total + value
            square = square + value * value
        cols[SUM_A, pl.ds(start, shard), :] = total
        cols[SUM_B, pl.ds(start, shard), :] = square
    chunked(second_sums)
    stat1 = stat_start(1, lane_sum(cols[SUM_A]), lane_sum(cols[SUM_B]))

    PAIR = 2 * channels

    def turn(full):
        depth = full.shape[2]
        for begin in range(0, depth, PAIR):
            end = min(begin + PAIR, depth)
            weights = full[:, :, begin:end].reshape(channels, end - begin)
            wturn[begin:end, :] = weights.T

    def conv_back(stack):
        def tile(at):
            total = jnp.zeros((channels, TILE), F32)
            for tap in range(9):
                span = slice(tap * channels, (tap + 1) * channels)
                total = total + jnp.dot(wturn[span, :], stack[span, at], preferred_element_type=F32)
            back[:, at] = total
        tiles(tile)

    pass2 = gather_pass(wfull2, gather2[1])
    gather2[0].wait_recv()
    pass2.wait_recv()
    turn(wfull2)
    conv_back(cot_stack)
    moments(1, stat1, 2)

    def second_act(start):
        at = pl.ds(start, shard)
        sums = [jnp.zeros((shard, LANES), F32)] * 2
        for h in range(height):
            normed = (normed2[at, line(h)] - cols[2, at, :]) * cols[3, at, :]
            normed2[at, line(h)] = normed
            pre = cols[10, at, :] * normed + cols[11, at, :]
            q = 1.0 / (1.0 + jnp.exp(-pre))
            act = (pre * q).astype(BF16).astype(F32)
            slope = back[at, line(h)] * (q * (1.0 + pre * (1.0 - q)))
            back[at, line(h)] = slope
            sums = [sums[0] + slope * normed, sums[1] + slope]
            put(mid_stack, act, start, h + 1, False)
            if h == 0:
                halo_out[1, 0, at, :] = act.astype(BF16)
            if h == height - 1:
                halo_out[1, 1, at, :] = act.astype(BF16)
        cols[SUM_C, at, :] = sums[0]
        cols[SUM_D, at, :] = sums[1]
    chunked(second_act)
    halo_b = halo_start(2, halo_out.at[1, 0], halo_out.at[1, 1])
    gain_cross2, bias_sum2 = lane_sum(cols[SUM_C]), lane_sum(cols[SUM_D])
    stat2 = stat_start(2, pv[:, 2:3] * bias_sum2, pv[:, 2:3] * gain_cross2)
    halo_finish(2, halo_b, mid_stack, False)

    depth = w1s.shape[1]

    def weight_grad(which, cot, stack):
        for begin in range(0, depth, PAIR):
            end = min(begin + PAIR, depth)
            value = lax.dot_general(
                cot[...], stack[begin:end, :], (((1,), (1,)), ((), ())), preferred_element_type=F32
            )
            part[which, :, :, begin:end] = value.astype(BF16).reshape(blocks, shard, end - begin)
        return [
            go(part.at[which, mate], core_in.at[which, 0], {"zero": mate}),
            go(part.at[which, over_mate], core_in.at[which, 1], {"zero": mate}),
        ]

    def reduce_core(which, copies):
        for copy in copies:
            copy.wait_recv()
        core_keep[which] = (
            part[which, over].astype(F32) + core_in[which, 1].astype(F32)
        ).astype(BF16)
        return go(core_keep.at[which], x_in.at[which], {"zero": over})

    piece = z_out.shape[3]

    def reduce_over(which, copy):
        copy.wait_recv()
        value = (
            part[which, zero].astype(F32)
            + core_in[which, 0].astype(F32)
            + x_in[which].astype(F32)
        ).astype(BF16)
        for q in range(-(-depth // piece)):
            end = min((q + 1) * piece, depth)
            z_out[which, q, :, : end - q * piece] = value[:, q * piece : end]
        copies = []
        for d in range(1, rows):
            to = lax.rem(row + d, rows)
            copies.append(go(z_out.at[which, to], z_in.at[which, row], {"rows": to}))
        return copies

    def reduce_rows(which, copies):
        for copy in copies:
            copy.wait_recv()
        z_in[which, row] = z_out[which, row]
        total = z_in[which, 0].astype(F32)
        for i in range(1, rows):
            total = total + z_in[which, i].astype(F32)
        z_all[which, row] = total.astype(BF16)
        return to_rows(z_all.at[which, row], z_all.at[which, row])

    def reduce_finish(which, copies, target):
        for copy in copies:
            copy.wait_recv()
        for q in range(-(-depth // piece)):
            end = min((q + 1) * piece, depth)
            target[:, q * piece : end] = z_all[which, q, :, : end - q * piece].astype(F32)

    grad2 = weight_grad(1, g, mid_stack)

    average, cross = stat_finish(2, stat2)
    column(4, average)
    column(5, cross)

    def hidden_back(start):
        at = pl.ds(start, shard)
        total = jnp.zeros((shard, LANES), F32)
        for h in range(height):
            value = cols[3, at, :] * (
                cols[10, at, :] * back[at, line(h)]
                - cols[4, at, :]
                - normed2[at, line(h)] * cols[5, at, :]
            )
            total = total + value
            rounded = value.astype(BF16)
            hgrad[at, line(h)] = rounded
            put(cot_stack, rounded.astype(F32), start, h + 1, True)
            if h == 0:
                halo_out[2, 0, at, :] = rounded
            if h == height - 1:
                halo_out[2, 1, at, :] = rounded
        cols[SUM_T, at, :] = total
    chunked(hidden_back)
    halo_h = halo_start(3, halo_out.at[2, 0], halo_out.at[2, 1])
    time_sum = lane_sum(cols[SUM_T])

    grad2 = reduce_core(1, grad2)
    grad1 = weight_grad(0, hgrad, act_stack)
    turn(wfull1)
    halo_finish(3, halo_h, cot_stack, True)
    conv_back(cot_stack)
    grad1 = reduce_core(0, grad1)
    grad2 = reduce_over(1, grad2)

    def first_slope(start):
        at = pl.ds(start, shard)
        sums = [jnp.zeros((shard, LANES), F32)] * 2
        for h in range(height):
            normed = normed1[at, line(h)]
            pre = cols[8, at, :] * normed + cols[9, at, :]
            q = 1.0 / (1.0 + jnp.exp(-pre))
            slope = back[at, line(h)] * (q * (1.0 + pre * (1.0 - q)))
            back[at, line(h)] = slope
            sums = [sums[0] + slope * normed, sums[1] + slope]
        cols[SUM_A, at, :] = sums[0]
        cols[SUM_B, at, :] = sums[1]
    chunked(first_slope)
    gain_cross1, bias_sum1 = lane_sum(cols[SUM_A]), lane_sum(cols[SUM_B])
    stat3 = stat_start(3, pv[:, 0:1] * bias_sum1, pv[:, 0:1] * gain_cross1)
    packed = jnp.zeros((channels, LANES), F32)
    for i, value in enumerate((time_sum, gain_cross1, bias_sum1, gain_cross2, bias_sum2)):
        packed = jnp.where(wide == i, value, packed)
    fill = jnp.zeros((tiny.shape[2] - channels, LANES), F32)
    tiny[row] = jnp.concatenate([packed, fill], axis=0).T[:8, :]
    tiny_rows = to_rows(tiny.at[row], tiny.at[row])

    def emit_out(at, value):
        out[:, at] = (x[:, at].astype(F32) + value).astype(BF16)
    conv(wfull2, mid_stack, emit_out)

    grad1 = reduce_over(0, grad1)
    average, cross = stat_finish(3, stat3)
    column(6, average)
    column(7, cross)

    for copy in tiny_rows:
        copy.wait_recv()
    total = tiny[0]
    for i in range(1, rows):
        total = total + tiny[i]
    tiny_x[0] = total
    first_hop = go(tiny_x.at[0], tiny_x.at[1], {"zero": mate})
    grad2 = reduce_rows(1, grad2)

    def input_back(start):
        at = pl.ds(start, shard)
        for h in range(height):
            value = cols[1, at, :] * (
                cols[8, at, :] * back[at, line(h)]
                - cols[6, at, :]
                - normed1[at, line(h)] * cols[7, at, :]
            )
            gin[at, line(h)] = (g[at, line(h)].astype(F32) + value).astype(BF16)
    chunked(input_back)

    first_hop.wait_recv()
    tiny_x[2] = total + tiny_x[1]
    second_hop = go(tiny_x.at[2], tiny_x.at[3], {"zero": over})
    grad1 = reduce_rows(0, grad1)
    second_hop.wait_recv()
    pick = lax.broadcasted_iota(jnp.int32, total.shape, 0)
    small[...] = jnp.where(pick == 0, total, tiny_x[2] + tiny_x[3])
    reduce_finish(1, grad2, dw2)
    reduce_finish(0, grad1, dw1)
    for copy in pending:
        copy.wait_send()


def local(latents, time_shift, conv_first, conv_second, norm_gains, norm_biases, grad_output):
    _, channels, height, width = latents.shape
    cells = height * width
    shard, taps, _ = conv_first.shape
    depth = taps * channels
    rows = lax.axis_size("rows")
    blocks = channels // shard
    vectors = jnp.stack(
        [norm_gains[0], norm_biases[0], norm_gains[1], norm_biases[1], time_shift[0]]
        + [jnp.zeros((channels,), F32)] * 3,
        axis=1,
    )
    group = jnp.arange(channels) // (channels // NORM_GROUPS)
    pool = (group[None, :] == jnp.arange(NORM_GROUPS)[:, None]).astype(F32)
    piece = -(-depth // (rows * LANES)) * LANES
    padded = -(-channels // LANES) * LANES
    vmem = pl.BlockSpec(memory_space=pltpu.VMEM)
    copies = 4 * (rows - 1) + 8 + 6 + 6 + 5 * (rows - 1) + 8
    field = jax.ShapeDtypeStruct((channels, cells), BF16)
    grads = jax.ShapeDtypeStruct((shard, depth), F32)
    out, gin, small, dw1, dw2 = pl.pallas_call(
        block_kernel,
        out_shape=(field, field, jax.ShapeDtypeStruct((8, padded), F32), grads, grads),
        in_specs=[vmem] * 7,
        out_specs=(vmem,) * 5,
        scratch_shapes=[
            pltpu.VMEM((depth, cells), BF16),
            pltpu.VMEM((depth, cells), BF16),
            pltpu.VMEM((depth, cells), BF16),
            pltpu.VMEM((blocks, shard, depth), BF16),
            pltpu.VMEM((blocks, shard, depth), BF16),
            pltpu.VMEM((depth, channels), BF16),
            pltpu.VMEM((channels, cells), F32),
            pltpu.VMEM((channels, cells), F32),
            pltpu.VMEM((channels, cells), F32),
            pltpu.VMEM((channels, cells), BF16),
            pltpu.VMEM((18, channels, LANES), F32),
            pltpu.VMEM((4, rows, NORM_GROUPS, LANES), F32),
            pltpu.VMEM((3, 2, channels, LANES), BF16),
            pltpu.VMEM((4, 2, channels, LANES), BF16),
            pltpu.VMEM((2, blocks, shard, depth), BF16),
            pltpu.VMEM((2, 2, shard, depth), BF16),
            pltpu.VMEM((2, shard, depth), BF16),
            pltpu.VMEM((2, shard, depth), BF16),
            pltpu.VMEM((2, rows, shard, piece), BF16),
            pltpu.VMEM((2, rows, shard, piece), BF16),
            pltpu.VMEM((2, rows, shard, piece), BF16),
            pltpu.VMEM((rows, 8, padded), F32),
            pltpu.VMEM((4, 8, padded), F32),
            pltpu.SemaphoreType.DMA((copies,)),
            pltpu.SemaphoreType.DMA((copies,)),
        ],
        compiler_params=pltpu.CompilerParams(
            collective_id=0, has_side_effects=True, vmem_limit_bytes=60 * 1024 * 1024
        ),
    )(
        latents.reshape(channels, cells),
        grad_output.reshape(channels, cells),
        vectors,
        conv_first.reshape(shard, depth),
        conv_second.reshape(shard, depth),
        pool,
        pool.T,
    )
    return (
        out.reshape(latents.shape),
        gin.reshape(latents.shape),
        small[0:1, :channels],
        dw1.reshape(conv_first.shape),
        dw2.reshape(conv_second.shape),
        small[1:5, :channels],
    )


def solution(mesh):
    placed = (
        P(("groups", "zero"), None, "rows", None),
        P(("groups", "zero"), None),
        P("zero", None, None),
        P("zero", None, None),
        P(),
        P(),
        P(("groups", "zero"), None, "rows", None),
    )
    return jax.shard_map(
        local,
        mesh=mesh,
        in_specs=placed,
        out_specs=(
            P(("groups", "zero"), None, "rows", None),
            P(("groups", "zero"), None, "rows", None),
            P(("groups", "zero"), None),
            P(("groups", "zero"), None, None),
            P(("groups", "zero"), None, None),
            P("groups", None),
        ),
        check_vma=False,
    )
```

```python
import jax
import jax.numpy as jnp
import numpy as np
from jax import lax
from jax.experimental import pallas as pl
from jax.experimental.pallas import tpu as pltpu
from jax.sharding import PartitionSpec as P

NORM_GROUPS = 32
EPSILON = 1e-05
LANES = 128
F32 = jnp.float32
BF16 = jnp.bfloat16
MESH = pl.DeviceIdType.MESH


def block_kernel(
    x, g, gains, biases, shift, w1s, w2s, pool, spread,
    out, gin, small, dw1, dw2,
    act_stack, mid_stack, cot_stack, wfull1, wfull2, wturn1, wturn2,
    normed1, normed2, back, hgrad, cols, stat, halo_out, halo_in,
    part, core_in, core_keep, x_in, z_out, z_in, z_all, flat, vectors, tiny, tiny_x,
    send, recv,
):
    channels, cells = x.shape
    height = cells // LANES
    taps, shard, _ = w1s.shape
    depth = taps * channels
    rows = lax.axis_size("rows")
    row = lax.axis_index("rows")
    zero = lax.axis_index("zero")
    core = lax.rem(zero, 2)
    mate = zero + 1 - 2 * core
    over = lax.rem(zero + 2, 4)
    over_mate = lax.rem(mate + 2, 4)
    blocks = channels // shard
    members = float(channels // NORM_GROUPS * cells * rows)
    lane = lax.broadcasted_iota(jnp.int32, (shard, LANES), 1)
    wide = lax.broadcasted_iota(jnp.int32, (channels, LANES), 1)
    counter = [0]

    def number():
        counter[0] += 1
        return counter[0] - 1

    pending = []

    def remote(src, dst, target):
        i = number()
        copy = pltpu.make_async_remote_copy(
            src_ref=src, dst_ref=dst, send_sem=send.at[i], recv_sem=recv.at[i],
            device_id=target, device_id_type=MESH,
        )
        return copy

    def go(src, dst, target):
        copy = remote(src, dst, target)
        copy.start()
        pending.append(copy)
        return copy

    def to_rows(src, dst):
        return [go(src, dst, {"rows": lax.rem(row + d, rows)}) for d in range(1, rows)]

    def chunked(body):
        def step(c, _):
            body(pl.multiple_of(c * shard, shard))
            return 0
        lax.fori_loop(0, blocks, step, 0)

    def put(stack, value, start, p, flip):
        left = jnp.where(lane == 0, 0.0, pltpu.roll(value, 1, 1)).astype(BF16)
        right = jnp.where(lane == LANES - 1, 0.0, pltpu.roll(value, LANES - 1, 1)).astype(BF16)
        slabs = (left, value.astype(BF16), right)
        for ty in range(3):
            h = p - 2 + ty if flip else p - ty
            if 0 <= h < height:
                for tx in range(3):
                    tap = 3 * ty + tx
                    stack[pl.ds(start + tap * channels, shard), h * LANES : (h + 1) * LANES] = (
                        slabs[2 - tx if flip else tx]
                    )

    def line(h):
        return slice(h * LANES, (h + 1) * LANES)

    def halo_start(stage, top, bottom):
        down = remote(bottom, halo_in.at[stage, 0], {"rows": lax.rem(row + 1, rows)})
        up = remote(top, halo_in.at[stage, 1], {"rows": lax.rem(row + rows - 1, rows)})

        @pl.when(row < rows - 1)
        def _():
            down.start()

        @pl.when(row > 0)
        def _():
            up.start()

        return down, up

    def halo_finish(stage, pair, stack, flip):
        down, up = pair

        @pl.when(row > 0)
        def _():
            down.wait_recv()
            up.wait_send()

        @pl.when(row < rows - 1)
        def _():
            up.wait_recv()
            down.wait_send()

        @pl.when(row == 0)
        def _():
            halo_in[stage, 0] = jnp.zeros((channels, LANES), BF16)

        @pl.when(row == rows - 1)
        def _():
            halo_in[stage, 1] = jnp.zeros((channels, LANES), BF16)

        def body(start):
            put(stack, halo_in[stage, 0, pl.ds(start, shard), :].astype(F32), start, 0, flip)
            put(stack, halo_in[stage, 1, pl.ds(start, shard), :].astype(F32), start, height + 1, flip)
        chunked(body)

    def lane_sum(value):
        return jnp.sum(value, axis=1, keepdims=True)

    def stat_start(stage, first, second):
        packed = jnp.where(wide == 0, first, jnp.where(wide == 1, second, 0.0))
        stat[stage, row] = jnp.dot(
            pool[...], packed, precision=lax.Precision.HIGHEST, preferred_element_type=F32
        )
        return to_rows(stat.at[stage, row], stat.at[stage, row])

    def stat_finish(stage, copies):
        for copy in copies:
            copy.wait_recv()
        total = stat[stage, 0]
        for i in range(1, rows):
            total = total + stat[stage, i]
        wide_total = jnp.dot(
            spread[...], total, precision=lax.Precision.HIGHEST, preferred_element_type=F32
        ) / members
        return wide_total[:, 0:1], wide_total[:, 1:2]

    def column(i, value):
        cols[i] = jnp.broadcast_to(value, (channels, LANES))

    def moments(stage, copies, at):
        average, square = stat_finish(stage, copies)
        column(at, average)
        column(at + 1, lax.rsqrt(square - average * average + EPSILON))

    barrier = pltpu.get_barrier_semaphore()
    for d in range(1, rows):
        pl.semaphore_signal(
            barrier, inc=1, device_id={"rows": lax.rem(row + d, rows)}, device_id_type=MESH
        )
    for target in (mate, over):
        pl.semaphore_signal(barrier, inc=1, device_id={"zero": target}, device_id_type=MESH)

    vectors[...] = jnp.zeros_like(vectors)
    vectors[0:2, 0:channels] = gains[...]
    vectors[2:4, 0:channels] = biases[...]
    vectors[4:5, 0:channels] = shift[...]
    pv = vectors[...].T[:channels, :]
    GAIN1, GAIN2 = pv[:, 0:1], pv[:, 1:2]
    SUM_A, SUM_B, SUM_C, SUM_D, SUM_T = 13, 14, 15, 16, 17
    for i in range(5):
        column((8, 10, 9, 11, 12)[i], pv[:, i : i + 1])

    def first_sums(start):
        total = jnp.zeros((shard, LANES), F32)
        square = total
        for h in range(height):
            value = x[pl.ds(start, shard), line(h)].astype(F32)
            total = total + value
            square = square + value * value
        cols[SUM_A, pl.ds(start, shard), :] = total
        cols[SUM_B, pl.ds(start, shard), :] = square
    chunked(first_sums)
    s0, s1 = lane_sum(cols[SUM_A]), lane_sum(cols[SUM_B])

    pl.semaphore_wait(barrier, rows - 1 + 2)
    stat0 = stat_start(0, s0, s1)
    halo_g = halo_start(0, g.at[:, 0:LANES], g.at[:, (height - 1) * LANES : height * LANES])

    def flatten(own, full):
        full[zero] = jnp.concatenate([own[tap] for tap in range(taps)], axis=1)

    def gather_start(full, target):
        return go(full.at[zero], full.at[zero], {"zero": target})

    def gather_pass(full, far):
        far.wait_recv()
        return go(full.at[over], full.at[over], {"zero": mate})

    flatten(w1s, wfull1)
    far1 = gather_start(wfull1, over)
    near1 = gather_start(wfull1, mate)
    flatten(w2s, wfull2)

    moments(0, stat0, 0)

    def first_act(start):
        at = pl.ds(start, shard)
        for h in range(height):
            normed = (x[at, line(h)].astype(F32) - cols[0, at, :]) * cols[1, at, :]
            normed1[at, line(h)] = normed
            pre = cols[8, at, :] * normed + cols[9, at, :]
            act = (pre / (1.0 + jnp.exp(-pre))).astype(BF16).astype(F32)
            put(act_stack, act, start, h + 1, False)
            if h == 0:
                halo_out[0, 0, at, :] = act.astype(BF16)
            if h == height - 1:
                halo_out[0, 1, at, :] = act.astype(BF16)
    chunked(first_act)
    halo_a = halo_start(1, halo_out.at[0, 0], halo_out.at[0, 1])

    def cot_fill(start):
        for h in range(height):
            put(cot_stack, g[pl.ds(start, shard), line(h)].astype(F32), start, h + 1, True)
    chunked(cot_fill)
    halo_finish(0, halo_g, cot_stack, True)
    pass1 = gather_pass(wfull1, far1)
    far2 = gather_start(wfull2, over)
    near2 = gather_start(wfull2, mate)
    halo_finish(1, halo_a, act_stack, False)
    near1.wait_recv()
    pass1.wait_recv()

    TILE = 256

    def tiles(body):
        def step(i, _):
            body(pl.ds(pl.multiple_of(i * TILE, TILE), TILE))
            return 0
        lax.fori_loop(0, cells // TILE, step, 0)

    def conv(full, stack, emit):
        def tile(at):
            weights = full[...].reshape(channels, full.shape[2])
            emit(at, jnp.dot(weights, stack[:, at], preferred_element_type=F32))
        tiles(tile)

    def emit_hidden(at, value):
        shift = cols[12][:, 0:1]
        normed2[:, at] = (value + shift).astype(BF16).astype(F32)
    conv(wfull1, act_stack, emit_hidden)

    def second_sums(start):
        total = jnp.zeros((shard, LANES), F32)
        square = total
        for h in range(height):
            value = normed2[pl.ds(start, shard), line(h)]
            total = total + value
            square = square + value * value
        cols[SUM_A, pl.ds(start, shard), :] = total
        cols[SUM_B, pl.ds(start, shard), :] = square
    chunked(second_sums)
    stat1 = stat_start(1, lane_sum(cols[SUM_A]), lane_sum(cols[SUM_B]))

    PAIR = 2 * channels

    def turn(full, wturn):
        for begin in range(0, depth, PAIR):
            end = min(begin + PAIR, depth)
            weights = full[:, :, begin:end].reshape(channels, end - begin)
            wturn[begin:end, :] = weights.T

    def conv_back(stack, wturn):
        def tile(at):
            total = jnp.zeros((channels, TILE), F32)
            for tap in range(9):
                span = slice(tap * channels, (tap + 1) * channels)
                total = total + jnp.dot(wturn[span, :], stack[span, at], preferred_element_type=F32)
            back[:, at] = total
        tiles(tile)

    pass2 = gather_pass(wfull2, far2)
    turn(wfull1, wturn1)
    near2.wait_recv()
    pass2.wait_recv()
    turn(wfull2, wturn2)
    conv_back(cot_stack, wturn2)
    moments(1, stat1, 2)

    def second_act(start):
        at = pl.ds(start, shard)
        sums = [jnp.zeros((shard, LANES), F32)] * 2
        for h in range(height):
            normed = (normed2[at, line(h)] - cols[2, at, :]) * cols[3, at, :]
            normed2[at, line(h)] = normed
            pre = cols[10, at, :] * normed + cols[11, at, :]
            q = 1.0 / (1.0 + jnp.exp(-pre))
            act = (pre * q).astype(BF16).astype(F32)
            slope = back[at, line(h)] * (q * (1.0 + pre * (1.0 - q)))
            back[at, line(h)] = slope
            sums = [sums[0] + slope * normed, sums[1] + slope]
            put(mid_stack, act, start, h + 1, False)
            if h == 0:
                halo_out[1, 0, at, :] = act.astype(BF16)
            if h == height - 1:
                halo_out[1, 1, at, :] = act.astype(BF16)
        cols[SUM_C, at, :] = sums[0]
        cols[SUM_D, at, :] = sums[1]
    chunked(second_act)
    halo_b = halo_start(2, halo_out.at[1, 0], halo_out.at[1, 1])
    gain_cross2, bias_sum2 = lane_sum(cols[SUM_C]), lane_sum(cols[SUM_D])
    stat2 = stat_start(2, GAIN2 * bias_sum2, GAIN2 * gain_cross2)
    halo_finish(2, halo_b, mid_stack, False)

    span = part.shape[3]
    piece = z_out.shape[3]
    steps = [1 << k for k in range(rows.bit_length() - 1)]

    def extent(stream):
        begin = stream % 2 * span
        return begin, min(begin + span, depth)

    def weight_grad(stream, cot, stack):
        first, last = extent(stream)
        half = span // 2
        for begin in range(first, last, half):
            end = min(begin + half, last)
            value = lax.dot_general(
                cot[...], stack[begin:end, :], (((1,), (1,)), ((), ())), preferred_element_type=F32
            )
            part[stream, :, :, begin - first : end - first] = value.astype(BF16).reshape(
                blocks, shard, end - begin
            )
        return [
            go(part.at[stream, over_mate], core_in.at[stream, 1], {"zero": mate}),
            go(part.at[stream, mate], core_in.at[stream, 0], {"zero": mate}),
        ]

    def reduce_core(stream, copies):
        copies[0].wait_recv()
        core_keep[stream] = (
            part[stream, over].astype(F32) + core_in[stream, 1].astype(F32)
        ).astype(BF16)
        return copies[1], go(core_keep.at[stream], x_in.at[stream], {"zero": over})

    def rows_send(stream, k, start, count):
        bit = lax.rem(lax.div(row, steps[k]), 2)
        half = count // 2
        keep = start + bit * half
        give = start + (1 - bit) * half
        offset = rows - count
        copy = go(
            z_out.at[stream, pl.ds(give, half)],
            z_in.at[stream, pl.ds(offset, half)],
            {"rows": row + steps[k] * (1 - 2 * bit)},
        )
        return copy, k, keep, half, offset

    def reduce_over(stream, copies):
        for copy in copies:
            copy.wait_recv()
        value = (
            part[stream, zero].astype(F32)
            + core_in[stream, 0].astype(F32)
            + x_in[stream].astype(F32)
        ).astype(BF16)
        for q in range(-(-span // piece)):
            z_out[stream, q] = value[:, q * piece : (q + 1) * piece]
        return rows_send(stream, 0, 0, rows)

    def reduce_step(stream, state):
        copy, k, keep, half, offset = state
        copy.wait_recv()
        last = k + 1 == len(steps)
        for i in range(half):
            value = (
                z_out[stream, keep + i].astype(F32) + z_in[stream, offset + i].astype(F32)
            ).astype(BF16)
            if last:
                z_all[stream, keep + i] = value
            else:
                z_out[stream, keep + i] = value
        if last:
            return gather_step(stream, k, keep, half)
        return rows_send(stream, k + 1, keep, half)

    def gather_step(stream, k, start, count):
        bit = lax.rem(lax.div(row, steps[k]), 2)
        at = pl.ds(start, count)
        copy = go(
            z_all.at[stream, at], z_all.at[stream, at], {"rows": row + steps[k] * (1 - 2 * bit)}
        )
        return copy, k, start - bit * count, 2 * count

    def spread_step(stream, state):
        copy, k, start, count = state
        copy.wait_recv()
        if k == 0:
            return None
        return gather_step(stream, k - 1, start, count)

    def reduce_finish(which, target):
        for stream in (2 * which, 2 * which + 1):
            first, last = extent(stream)
            for q in range(-(-(last - first) // piece)):
                begin = first + q * piece
                flat[which, :, begin : begin + piece] = z_all[stream, q].astype(F32)
        for tap in range(taps):
            target[tap] = flat[which, :, tap * channels : (tap + 1) * channels]

    s2 = weight_grad(2, g, mid_stack)
    s3 = weight_grad(3, g, mid_stack)

    average, cross = stat_finish(2, stat2)
    column(4, average)
    column(5, cross)

    def hidden_back(start):
        at = pl.ds(start, shard)
        total = jnp.zeros((shard, LANES), F32)
        for h in range(height):
            value = cols[3, at, :] * (
                cols[10, at, :] * back[at, line(h)]
                - cols[4, at, :]
                - normed2[at, line(h)] * cols[5, at, :]
            )
            total = total + value
            rounded = value.astype(BF16)
            hgrad[at, line(h)] = rounded
            put(cot_stack, rounded.astype(F32), start, h + 1, True)
            if h == 0:
                halo_out[2, 0, at, :] = rounded
            if h == height - 1:
                halo_out[2, 1, at, :] = rounded
        cols[SUM_T, at, :] = total
    chunked(hidden_back)
    halo_h = halo_start(3, halo_out.at[2, 0], halo_out.at[2, 1])
    time_sum = lane_sum(cols[SUM_T])

    s2 = reduce_core(2, s2)
    s3 = reduce_core(3, s3)
    s0 = weight_grad(0, hgrad, act_stack)
    s2 = reduce_over(2, s2)
    s1 = weight_grad(1, hgrad, act_stack)
    s0 = reduce_core(0, s0)
    s3 = reduce_over(3, s3)
    halo_finish(3, halo_h, cot_stack, True)
    s1 = reduce_core(1, s1)
    s2 = reduce_step(2, s2)
    conv_back(cot_stack, wturn1)
    s0 = reduce_over(0, s0)
    s3 = reduce_step(3, s3)
    for _ in steps[1:]:
        s2 = reduce_step(2, s2)
    s1 = reduce_over(1, s1)
    for _ in steps[1:]:
        s3 = reduce_step(3, s3)

    def first_slope(start):
        at = pl.ds(start, shard)
        sums = [jnp.zeros((shard, LANES), F32)] * 2
        for h in range(height):
            normed = normed1[at, line(h)]
            pre = cols[8, at, :] * normed + cols[9, at, :]
            q = 1.0 / (1.0 + jnp.exp(-pre))
            slope = back[at, line(h)] * (q * (1.0 + pre * (1.0 - q)))
            back[at, line(h)] = slope
            sums = [sums[0] + slope * normed, sums[1] + slope]
        cols[SUM_A, at, :] = sums[0]
        cols[SUM_B, at, :] = sums[1]
    chunked(first_slope)
    gain_cross1, bias_sum1 = lane_sum(cols[SUM_A]), lane_sum(cols[SUM_B])
    stat3 = stat_start(3, GAIN1 * bias_sum1, GAIN1 * gain_cross1)
    packed = jnp.zeros((channels, LANES), F32)
    for i, value in enumerate((time_sum, gain_cross1, bias_sum1, gain_cross2, bias_sum2)):
        packed = jnp.where(wide == i, value, packed)
    fill = jnp.zeros((tiny.shape[2] - channels, LANES), F32)
    tiny[row] = jnp.concatenate([packed, fill], axis=0).T[:8, :]
    tiny_rows = to_rows(tiny.at[row], tiny.at[row])

    def emit_out(at, value):
        out[:, at] = (x[:, at].astype(F32) + value).astype(BF16)
    conv(wfull2, mid_stack, emit_out)

    s0 = reduce_step(0, s0)
    s1 = reduce_step(1, s1)
    average, cross = stat_finish(3, stat3)
    column(6, average)
    column(7, cross)

    for copy in tiny_rows:
        copy.wait_recv()
    total = tiny[0]
    for i in range(1, rows):
        total = total + tiny[i]
    tiny_x[0] = total
    first_hop = go(tiny_x.at[0], tiny_x.at[1], {"zero": mate})
    for _ in steps[1:]:
        s0 = reduce_step(0, s0)
        s1 = reduce_step(1, s1)
    s2 = spread_step(2, s2)
    s3 = spread_step(3, s3)

    def input_back(start):
        at = pl.ds(start, shard)
        for h in range(height):
            value = cols[1, at, :] * (
                cols[8, at, :] * back[at, line(h)]
                - cols[6, at, :]
                - normed1[at, line(h)] * cols[7, at, :]
            )
            gin[at, line(h)] = (g[at, line(h)].astype(F32) + value).astype(BF16)
    chunked(input_back)

    first_hop.wait_recv()
    tiny_x[2] = total + tiny_x[1]
    second_hop = go(tiny_x.at[2], tiny_x.at[3], {"zero": over})
    for _ in steps[1:]:
        s2 = spread_step(2, s2)
        s3 = spread_step(3, s3)
    s0 = spread_step(0, s0)
    s1 = spread_step(1, s1)
    reduce_finish(1, dw2)
    second_hop.wait_recv()
    pick = lax.broadcasted_iota(jnp.int32, total.shape, 0)
    small[...] = jnp.where(pick == 0, total, tiny_x[2] + tiny_x[3])
    for _ in steps[1:]:
        s0 = spread_step(0, s0)
        s1 = spread_step(1, s1)
    reduce_finish(0, dw1)
    for copy in pending:
        copy.wait_send()


def local(latents, time_shift, conv_first, conv_second, norm_gains, norm_biases, grad_output):
    _, channels, height, width = latents.shape
    cells = height * width
    shard, taps, _ = conv_first.shape
    depth = taps * channels
    rows = lax.axis_size("rows")
    blocks = channels // shard
    group = np.arange(channels) // (channels // NORM_GROUPS)
    pool = (group[None, :] == np.arange(NORM_GROUPS)[:, None]).astype(np.float32)
    levels = rows.bit_length() - 1
    span = -(-depth // (8 * LANES)) * 4 * LANES
    piece = -(-span // (rows * LANES)) * LANES
    padded = -(-channels // LANES) * LANES
    vmem = pl.BlockSpec(memory_space=pltpu.VMEM)
    copies = 5 * (rows - 1) + 8 + 6 + 4 * (3 + 2 * levels) + 2
    field = jax.ShapeDtypeStruct((channels, cells), BF16)
    grads = jax.ShapeDtypeStruct((taps, shard, channels), F32)
    out, gin, small, dw1, dw2 = pl.pallas_call(
        block_kernel,
        out_shape=(field, field, jax.ShapeDtypeStruct((8, padded), F32), grads, grads),
        in_specs=[vmem] * 9,
        out_specs=(vmem,) * 5,
        scratch_shapes=[
            pltpu.VMEM((depth, cells), BF16),
            pltpu.VMEM((depth, cells), BF16),
            pltpu.VMEM((depth, cells), BF16),
            pltpu.VMEM((blocks, shard, depth), BF16),
            pltpu.VMEM((blocks, shard, depth), BF16),
            pltpu.VMEM((depth, channels), BF16),
            pltpu.VMEM((depth, channels), BF16),
            pltpu.VMEM((channels, cells), F32),
            pltpu.VMEM((channels, cells), F32),
            pltpu.VMEM((channels, cells), F32),
            pltpu.VMEM((channels, cells), BF16),
            pltpu.VMEM((18, channels, LANES), F32),
            pltpu.VMEM((4, rows, NORM_GROUPS, LANES), F32),
            pltpu.VMEM((3, 2, channels, LANES), BF16),
            pltpu.VMEM((4, 2, channels, LANES), BF16),
            pltpu.VMEM((4, blocks, shard, span), BF16),
            pltpu.VMEM((4, 2, shard, span), BF16),
            pltpu.VMEM((4, shard, span), BF16),
            pltpu.VMEM((4, shard, span), BF16),
            pltpu.VMEM((4, rows, shard, piece), BF16),
            pltpu.VMEM((4, rows, shard, piece), BF16),
            pltpu.VMEM((4, rows, shard, piece), BF16),
            pltpu.VMEM((2, shard, 2 * span), F32),
            pltpu.VMEM((LANES, padded), F32),
            pltpu.VMEM((rows, 8, padded), F32),
            pltpu.VMEM((4, 8, padded), F32),
            pltpu.SemaphoreType.DMA((copies,)),
            pltpu.SemaphoreType.DMA((copies,)),
        ],
        compiler_params=pltpu.CompilerParams(
            collective_id=0, has_side_effects=True, vmem_limit_bytes=60 * 1024 * 1024
        ),
    )(
        latents.reshape(channels, cells),
        grad_output.reshape(channels, cells),
        norm_gains,
        norm_biases,
        time_shift,
        jnp.transpose(conv_first, (1, 0, 2)),
        jnp.transpose(conv_second, (1, 0, 2)),
        jnp.asarray(pool),
        jnp.asarray(np.ascontiguousarray(pool.T)),
    )
    return (
        out.reshape(latents.shape),
        gin.reshape(latents.shape),
        small[0:1, :channels],
        jnp.transpose(dw1, (1, 0, 2)),
        jnp.transpose(dw2, (1, 0, 2)),
        small[1:5, :channels],
    )


def solution(mesh):
    placed = (
        P(("groups", "zero"), None, "rows", None),
        P(("groups", "zero"), None),
        P("zero", None, None),
        P("zero", None, None),
        P(),
        P(),
        P(("groups", "zero"), None, "rows", None),
    )
    return jax.shard_map(
        local,
        mesh=mesh,
        in_specs=placed,
        out_specs=(
            P(("groups", "zero"), None, "rows", None),
            P(("groups", "zero"), None, "rows", None),
            P(("groups", "zero"), None),
            P(("groups", "zero"), None, None),
            P(("groups", "zero"), None, None),
            P("groups", None),
        ),
        check_vma=False,
    )
```

```python
import jax
import jax.numpy as jnp
import numpy as np
from jax import lax
from jax.experimental import pallas as pl
from jax.experimental.pallas import tpu as pltpu
from jax.sharding import PartitionSpec as P

NORM_GROUPS = 32
EPSILON = 1e-05
LANES = 128
F32 = jnp.float32
BF16 = jnp.bfloat16
MESH = pl.DeviceIdType.MESH


def block_kernel(
    x, g, gains, biases, shift, w1s, w2s, pool, spread,
    out, gin, small, dw1, dw2,
    act_stack, mid_stack, cot_stack, wfull1, wfull2, wturn1, wturn2,
    normed1, normed2, back, hgrad, cols, stat, halo_out, halo_in,
    part, core_in, core_keep, x_in, z_out, z_in, z_all, flat, vectors, tiny, tiny_x,
    send, recv,
):
    channels, cells = x.shape
    height = cells // LANES
    taps, shard, _ = w1s.shape
    depth = taps * channels
    rows = lax.axis_size("rows")
    row = lax.axis_index("rows")
    zero = lax.axis_index("zero")
    core = lax.rem(zero, 2)
    mate = zero + 1 - 2 * core
    over = lax.rem(zero + 2, 4)
    over_mate = lax.rem(mate + 2, 4)
    blocks = channels // shard
    members = float(channels // NORM_GROUPS * cells * rows)
    lane = lax.broadcasted_iota(jnp.int32, (shard, LANES), 1)
    wide = lax.broadcasted_iota(jnp.int32, (channels, LANES), 1)
    counter = [0]

    def number():
        counter[0] += 1
        return counter[0] - 1

    pending = []

    def remote(src, dst, target):
        i = number()
        copy = pltpu.make_async_remote_copy(
            src_ref=src, dst_ref=dst, send_sem=send.at[i], recv_sem=recv.at[i],
            device_id=target, device_id_type=MESH,
        )
        return copy

    def go(src, dst, target):
        copy = remote(src, dst, target)
        copy.start()
        pending.append(copy)
        return copy

    def to_rows(src, dst):
        return [go(src, dst, {"rows": lax.rem(row + d, rows)}) for d in range(1, rows)]

    def chunked(body):
        def step(c, _):
            body(pl.multiple_of(c * shard, shard))
            return 0
        lax.fori_loop(0, blocks, step, 0)

    def put(stack, value, start, p, flip):
        left = jnp.where(lane == 0, 0.0, pltpu.roll(value, 1, 1)).astype(BF16)
        right = jnp.where(lane == LANES - 1, 0.0, pltpu.roll(value, LANES - 1, 1)).astype(BF16)
        slabs = (left, value.astype(BF16), right)
        for ty in range(3):
            h = p - 2 + ty if flip else p - ty
            if 0 <= h < height:
                for tx in range(3):
                    tap = 3 * ty + tx
                    stack[pl.ds(start + tap * channels, shard), h * LANES : (h + 1) * LANES] = (
                        slabs[2 - tx if flip else tx]
                    )

    def line(h):
        return slice(h * LANES, (h + 1) * LANES)

    def halo_start(stage, top, bottom):
        down = remote(bottom, halo_in.at[stage, 0], {"rows": lax.rem(row + 1, rows)})
        up = remote(top, halo_in.at[stage, 1], {"rows": lax.rem(row + rows - 1, rows)})

        @pl.when(row < rows - 1)
        def _():
            down.start()

        @pl.when(row > 0)
        def _():
            up.start()

        return down, up

    def halo_finish(stage, pair, stack, flip):
        down, up = pair

        @pl.when(row > 0)
        def _():
            down.wait_recv()
            up.wait_send()

        @pl.when(row < rows - 1)
        def _():
            up.wait_recv()
            down.wait_send()

        @pl.when(row == 0)
        def _():
            halo_in[stage, 0] = jnp.zeros((channels, LANES), BF16)

        @pl.when(row == rows - 1)
        def _():
            halo_in[stage, 1] = jnp.zeros((channels, LANES), BF16)

        def body(start):
            put(stack, halo_in[stage, 0, pl.ds(start, shard), :].astype(F32), start, 0, flip)
            put(stack, halo_in[stage, 1, pl.ds(start, shard), :].astype(F32), start, height + 1, flip)
        chunked(body)

    def lane_sum(value):
        return jnp.sum(value, axis=1, keepdims=True)

    def stat_start(stage, first, second):
        packed = jnp.where(wide == 0, first, jnp.where(wide == 1, second, 0.0))
        stat[stage, row] = jnp.dot(
            pool[...], packed, precision=lax.Precision.HIGHEST, preferred_element_type=F32
        )
        return to_rows(stat.at[stage, row], stat.at[stage, row])

    def stat_finish(stage, copies):
        for copy in copies:
            copy.wait_recv()
        total = stat[stage, 0]
        for i in range(1, rows):
            total = total + stat[stage, i]
        wide_total = jnp.dot(
            spread[...], total, precision=lax.Precision.HIGHEST, preferred_element_type=F32
        ) / members
        return wide_total[:, 0:1], wide_total[:, 1:2]

    def column(i, value):
        cols[i] = jnp.broadcast_to(value, (channels, LANES))

    def moments(stage, copies, at):
        average, square = stat_finish(stage, copies)
        column(at, average)
        column(at + 1, lax.rsqrt(square - average * average + EPSILON))

    barrier = pltpu.get_barrier_semaphore()
    for d in range(1, rows):
        pl.semaphore_signal(
            barrier, inc=1, device_id={"rows": lax.rem(row + d, rows)}, device_id_type=MESH
        )
    for target in (mate, over):
        pl.semaphore_signal(barrier, inc=1, device_id={"zero": target}, device_id_type=MESH)

    vectors[...] = jnp.zeros_like(vectors)
    vectors[0:2, 0:channels] = gains[...]
    vectors[2:4, 0:channels] = biases[...]
    vectors[4:5, 0:channels] = shift[...]
    pv = vectors[...].T[:channels, :]
    GAIN1, GAIN2 = pv[:, 0:1], pv[:, 1:2]
    SUM_A, SUM_B, SUM_C, SUM_D, SUM_T = 13, 14, 15, 16, 17
    for i in range(5):
        column((8, 10, 9, 11, 12)[i], pv[:, i : i + 1])

    def first_sums(start):
        total = jnp.zeros((shard, LANES), F32)
        square = total
        for h in range(height):
            value = x[pl.ds(start, shard), line(h)].astype(F32)
            total = total + value
            square = square + value * value
        cols[SUM_A, pl.ds(start, shard), :] = total
        cols[SUM_B, pl.ds(start, shard), :] = square
    chunked(first_sums)
    s0, s1 = lane_sum(cols[SUM_A]), lane_sum(cols[SUM_B])

    pl.semaphore_wait(barrier, rows - 1 + 2)
    stat0 = stat_start(0, s0, s1)
    halo_g = halo_start(0, g.at[:, 0:LANES], g.at[:, (height - 1) * LANES : height * LANES])

    def flatten(own, full):
        full[zero] = jnp.concatenate([own[tap] for tap in range(taps)], axis=1)

    def gather_start(full, target):
        return go(full.at[zero], full.at[zero], {"zero": target})

    def gather_pass(full, far):
        far.wait_recv()
        return go(full.at[over], full.at[over], {"zero": mate})

    flatten(w1s, wfull1)
    far1 = gather_start(wfull1, over)
    near1 = gather_start(wfull1, mate)
    flatten(w2s, wfull2)

    moments(0, stat0, 0)

    def first_act(start):
        at = pl.ds(start, shard)
        for h in range(height):
            normed = (x[at, line(h)].astype(F32) - cols[0, at, :]) * cols[1, at, :]
            normed1[at, line(h)] = normed
            pre = cols[8, at, :] * normed + cols[9, at, :]
            act = (pre / (1.0 + jnp.exp(-pre))).astype(BF16).astype(F32)
            put(act_stack, act, start, h + 1, False)
            if h == 0:
                halo_out[0, 0, at, :] = act.astype(BF16)
            if h == height - 1:
                halo_out[0, 1, at, :] = act.astype(BF16)
    chunked(first_act)
    halo_a = halo_start(1, halo_out.at[0, 0], halo_out.at[0, 1])

    def cot_fill(start):
        for h in range(height):
            put(cot_stack, g[pl.ds(start, shard), line(h)].astype(F32), start, h + 1, True)
    chunked(cot_fill)
    halo_finish(0, halo_g, cot_stack, True)
    pass1 = gather_pass(wfull1, far1)
    far2 = gather_start(wfull2, over)
    near2 = gather_start(wfull2, mate)
    halo_finish(1, halo_a, act_stack, False)
    near1.wait_recv()
    pass1.wait_recv()

    TILE = 256

    count = cells // TILE

    def tiles(body, first=0, last=count):
        def step(i, _):
            body(pl.ds(pl.multiple_of(i * TILE, TILE), TILE))
            return 0
        lax.fori_loop(first, last, step, 0)

    def conv(full, stack, emit, first=0, last=count):
        def tile(at):
            weights = full[...].reshape(channels, full.shape[2])
            emit(at, jnp.dot(weights, stack[:, at], preferred_element_type=F32))
        tiles(tile, first, last)

    def emit_hidden(at, value):
        shift = cols[12][:, 0:1]
        normed2[:, at] = (value + shift).astype(BF16).astype(F32)
    conv(wfull1, act_stack, emit_hidden)

    def second_sums(start):
        total = jnp.zeros((shard, LANES), F32)
        square = total
        for h in range(height):
            value = normed2[pl.ds(start, shard), line(h)]
            total = total + value
            square = square + value * value
        cols[SUM_A, pl.ds(start, shard), :] = total
        cols[SUM_B, pl.ds(start, shard), :] = square
    chunked(second_sums)
    stat1 = stat_start(1, lane_sum(cols[SUM_A]), lane_sum(cols[SUM_B]))

    PAIR = 2 * channels

    def turn(full, wturn):
        for begin in range(0, depth, PAIR):
            end = min(begin + PAIR, depth)
            weights = full[:, :, begin:end].reshape(channels, end - begin)
            turned = weights.T
            wturn[:, begin:end] = jnp.concatenate(
                [turned[i : i + channels] for i in range(0, end - begin, channels)], axis=1
            )

    def conv_back(stack, wturn):
        def tile(at):
            total = jnp.dot(wturn[...], stack[:, at], preferred_element_type=F32)
            back[:, at] = total
        tiles(tile)

    pass2 = gather_pass(wfull2, far2)
    turn(wfull1, wturn1)
    near2.wait_recv()
    pass2.wait_recv()
    turn(wfull2, wturn2)
    conv_back(cot_stack, wturn2)
    moments(1, stat1, 2)

    def second_act(start):
        at = pl.ds(start, shard)
        sums = [jnp.zeros((shard, LANES), F32)] * 2
        for h in range(height):
            normed = (normed2[at, line(h)] - cols[2, at, :]) * cols[3, at, :]
            normed2[at, line(h)] = normed
            pre = cols[10, at, :] * normed + cols[11, at, :]
            q = 1.0 / (1.0 + jnp.exp(-pre))
            act = (pre * q).astype(BF16).astype(F32)
            slope = back[at, line(h)] * (q * (1.0 + pre * (1.0 - q)))
            back[at, line(h)] = slope
            sums = [sums[0] + slope * normed, sums[1] + slope]
            put(mid_stack, act, start, h + 1, False)
            if h == 0:
                halo_out[1, 0, at, :] = act.astype(BF16)
            if h == height - 1:
                halo_out[1, 1, at, :] = act.astype(BF16)
        cols[SUM_C, at, :] = sums[0]
        cols[SUM_D, at, :] = sums[1]
    chunked(second_act)
    halo_b = halo_start(2, halo_out.at[1, 0], halo_out.at[1, 1])
    gain_cross2, bias_sum2 = lane_sum(cols[SUM_C]), lane_sum(cols[SUM_D])
    stat2 = stat_start(2, GAIN2 * bias_sum2, GAIN2 * gain_cross2)
    halo_finish(2, halo_b, mid_stack, False)

    span = part.shape[3]
    piece = z_out.shape[3]
    steps = [1 << k for k in range(rows.bit_length() - 1)]

    def extent(stream):
        begin = stream % 2 * span
        return begin, min(begin + span, depth)

    def weight_grad(stream, cot, stack):
        first, last = extent(stream)
        half = span // 2
        for begin in range(first, last, half):
            end = min(begin + half, last)
            value = lax.dot_general(
                cot[...], stack[begin:end, :], (((1,), (1,)), ((), ())), preferred_element_type=F32
            )
            part[stream, :, :, begin - first : end - first] = value.astype(BF16).reshape(
                blocks, shard, end - begin
            )
        return [
            go(part.at[stream, over_mate], core_in.at[stream, 1], {"zero": mate}),
            go(part.at[stream, mate], core_in.at[stream, 0], {"zero": mate}),
        ]

    def reduce_core(stream, copies):
        copies[0].wait_recv()
        core_keep[stream] = (
            part[stream, over].astype(F32) + core_in[stream, 1].astype(F32)
        ).astype(BF16)
        return copies[1], go(core_keep.at[stream], x_in.at[stream], {"zero": over})

    def rows_send(stream, k, start, count):
        bit = lax.rem(lax.div(row, steps[k]), 2)
        half = count // 2
        keep = start + bit * half
        give = start + (1 - bit) * half
        offset = rows - count
        copy = go(
            z_out.at[stream, pl.ds(give, half)],
            z_in.at[stream, pl.ds(offset, half)],
            {"rows": row + steps[k] * (1 - 2 * bit)},
        )
        return copy, k, keep, half, offset

    def reduce_over(stream, copies):
        for copy in copies:
            copy.wait_recv()
        value = (
            part[stream, zero].astype(F32)
            + core_in[stream, 0].astype(F32)
            + x_in[stream].astype(F32)
        ).astype(BF16)
        for q in range(-(-span // piece)):
            z_out[stream, q] = value[:, q * piece : (q + 1) * piece]
        return rows_send(stream, 0, 0, rows)

    def reduce_step(stream, state):
        copy, k, keep, half, offset = state
        copy.wait_recv()
        last = k + 1 == len(steps)
        for i in range(half):
            value = (
                z_out[stream, keep + i].astype(F32) + z_in[stream, offset + i].astype(F32)
            ).astype(BF16)
            if last:
                z_all[stream, keep + i] = value
            else:
                z_out[stream, keep + i] = value
        if last:
            return gather_step(stream, k, keep, half)
        return rows_send(stream, k + 1, keep, half)

    def gather_step(stream, k, start, count):
        bit = lax.rem(lax.div(row, steps[k]), 2)
        at = pl.ds(start, count)
        copy = go(
            z_all.at[stream, at], z_all.at[stream, at], {"rows": row + steps[k] * (1 - 2 * bit)}
        )
        return copy, k, start - bit * count, 2 * count

    def spread_step(stream, state):
        copy, k, start, count = state
        copy.wait_recv()
        if k == 0:
            return None
        return gather_step(stream, k - 1, start, count)

    def reduce_finish(which, target):
        for stream in (2 * which, 2 * which + 1):
            first, last = extent(stream)
            for q in range(-(-(last - first) // piece)):
                begin = first + q * piece
                flat[which, :, begin : begin + piece] = z_all[stream, q].astype(F32)
        for tap in range(taps):
            target[tap] = flat[which, :, tap * channels : (tap + 1) * channels]

    s2 = weight_grad(2, g, mid_stack)
    s3 = weight_grad(3, g, mid_stack)

    average, cross = stat_finish(2, stat2)
    column(4, average)
    column(5, cross)

    def hidden_back(start):
        at = pl.ds(start, shard)
        total = jnp.zeros((shard, LANES), F32)
        for h in range(height):
            value = cols[3, at, :] * (
                cols[10, at, :] * back[at, line(h)]
                - cols[4, at, :]
                - normed2[at, line(h)] * cols[5, at, :]
            )
            total = total + value
            rounded = value.astype(BF16)
            hgrad[at, line(h)] = rounded
            put(cot_stack, rounded.astype(F32), start, h + 1, True)
            if h == 0:
                halo_out[2, 0, at, :] = rounded
            if h == height - 1:
                halo_out[2, 1, at, :] = rounded
        cols[SUM_T, at, :] = total
    chunked(hidden_back)
    halo_h = halo_start(3, halo_out.at[2, 0], halo_out.at[2, 1])
    time_sum = lane_sum(cols[SUM_T])

    s2 = reduce_core(2, s2)
    s3 = reduce_core(3, s3)
    s0 = weight_grad(0, hgrad, act_stack)
    s2 = reduce_over(2, s2)
    s1 = weight_grad(1, hgrad, act_stack)
    s0 = reduce_core(0, s0)
    s3 = reduce_over(3, s3)
    halo_finish(3, halo_h, cot_stack, True)
    s1 = reduce_core(1, s1)
    s2 = reduce_step(2, s2)
    conv_back(cot_stack, wturn1)
    s0 = reduce_over(0, s0)
    s3 = reduce_step(3, s3)
    for _ in steps[1:]:
        s2 = reduce_step(2, s2)

    def first_slope(start):
        at = pl.ds(start, shard)
        sums = [jnp.zeros((shard, LANES), F32)] * 2
        for h in range(height):
            normed = normed1[at, line(h)]
            pre = cols[8, at, :] * normed + cols[9, at, :]
            q = 1.0 / (1.0 + jnp.exp(-pre))
            slope = back[at, line(h)] * (q * (1.0 + pre * (1.0 - q)))
            back[at, line(h)] = slope
            sums = [sums[0] + slope * normed, sums[1] + slope]
        cols[SUM_A, at, :] = sums[0]
        cols[SUM_B, at, :] = sums[1]
    chunked(first_slope)
    gain_cross1, bias_sum1 = lane_sum(cols[SUM_A]), lane_sum(cols[SUM_B])
    stat3 = stat_start(3, GAIN1 * bias_sum1, GAIN1 * gain_cross1)
    s1 = reduce_over(1, s1)
    s0 = reduce_step(0, s0)
    for _ in steps[1:]:
        s3 = reduce_step(3, s3)
    packed = jnp.zeros((channels, LANES), F32)
    for i, value in enumerate((time_sum, gain_cross1, bias_sum1, gain_cross2, bias_sum2)):
        packed = jnp.where(wide == i, value, packed)
    fill = jnp.zeros((tiny.shape[2] - channels, LANES), F32)
    tiny[row] = jnp.concatenate([packed, fill], axis=0).T[:8, :]
    tiny_rows = to_rows(tiny.at[row], tiny.at[row])

    def emit_out(at, value):
        out[:, at] = (x[:, at].astype(F32) + value).astype(BF16)
    conv(wfull2, mid_stack, emit_out, 0, count // 2)
    s1 = reduce_step(1, s1)
    for _ in steps[1:]:
        s0 = reduce_step(0, s0)
    s2 = spread_step(2, s2)
    conv(wfull2, mid_stack, emit_out, count // 2, count)
    for _ in steps[1:]:
        s1 = reduce_step(1, s1)
    s3 = spread_step(3, s3)
    s0 = spread_step(0, s0)

    average, cross = stat_finish(3, stat3)
    column(6, average)
    column(7, cross)

    for copy in tiny_rows:
        copy.wait_recv()
    total = tiny[0]
    for i in range(1, rows):
        total = total + tiny[i]
    tiny_x[0] = total
    first_hop = go(tiny_x.at[0], tiny_x.at[1], {"zero": mate})
    def input_back(start):
        at = pl.ds(start, shard)
        for h in range(height):
            value = cols[1, at, :] * (
                cols[8, at, :] * back[at, line(h)]
                - cols[6, at, :]
                - normed1[at, line(h)] * cols[7, at, :]
            )
            gin[at, line(h)] = (g[at, line(h)].astype(F32) + value).astype(BF16)
    chunked(input_back)

    first_hop.wait_recv()
    tiny_x[2] = total + tiny_x[1]
    second_hop = go(tiny_x.at[2], tiny_x.at[3], {"zero": over})
    for _ in steps[1:]:
        s2 = spread_step(2, s2)
        s3 = spread_step(3, s3)
    s1 = spread_step(1, s1)
    reduce_finish(1, dw2)
    second_hop.wait_recv()
    pick = lax.broadcasted_iota(jnp.int32, total.shape, 0)
    small[...] = jnp.where(pick == 0, total, tiny_x[2] + tiny_x[3])
    for _ in steps[1:]:
        s0 = spread_step(0, s0)
        s1 = spread_step(1, s1)
    reduce_finish(0, dw1)
    for copy in pending:
        copy.wait_send()


def local(latents, time_shift, conv_first, conv_second, norm_gains, norm_biases, grad_output):
    _, channels, height, width = latents.shape
    cells = height * width
    shard, taps, _ = conv_first.shape
    depth = taps * channels
    rows = lax.axis_size("rows")
    blocks = channels // shard
    group = np.arange(channels) // (channels // NORM_GROUPS)
    pool = (group[None, :] == np.arange(NORM_GROUPS)[:, None]).astype(np.float32)
    levels = rows.bit_length() - 1
    span = -(-depth // (8 * LANES)) * 4 * LANES
    piece = -(-span // (rows * LANES)) * LANES
    padded = -(-channels // LANES) * LANES
    vmem = pl.BlockSpec(memory_space=pltpu.VMEM)
    copies = 5 * (rows - 1) + 8 + 6 + 4 * (3 + 2 * levels) + 2
    field = jax.ShapeDtypeStruct((channels, cells), BF16)
    grads = jax.ShapeDtypeStruct((taps, shard, channels), F32)
    out, gin, small, dw1, dw2 = pl.pallas_call(
        block_kernel,
        out_shape=(field, field, jax.ShapeDtypeStruct((8, padded), F32), grads, grads),
        in_specs=[vmem] * 9,
        out_specs=(vmem,) * 5,
        scratch_shapes=[
            pltpu.VMEM((depth, cells), BF16),
            pltpu.VMEM((depth, cells), BF16),
            pltpu.VMEM((depth, cells), BF16),
            pltpu.VMEM((blocks, shard, depth), BF16),
            pltpu.VMEM((blocks, shard, depth), BF16),
            pltpu.VMEM((channels, depth), BF16),
            pltpu.VMEM((channels, depth), BF16),
            pltpu.VMEM((channels, cells), F32),
            pltpu.VMEM((channels, cells), F32),
            pltpu.VMEM((channels, cells), F32),
            pltpu.VMEM((channels, cells), BF16),
            pltpu.VMEM((18, channels, LANES), F32),
            pltpu.VMEM((4, rows, NORM_GROUPS, LANES), F32),
            pltpu.VMEM((3, 2, channels, LANES), BF16),
            pltpu.VMEM((4, 2, channels, LANES), BF16),
            pltpu.VMEM((4, blocks, shard, span), BF16),
            pltpu.VMEM((4, 2, shard, span), BF16),
            pltpu.VMEM((4, shard, span), BF16),
            pltpu.VMEM((4, shard, span), BF16),
            pltpu.VMEM((4, rows, shard, piece), BF16),
            pltpu.VMEM((4, rows, shard, piece), BF16),
            pltpu.VMEM((4, rows, shard, piece), BF16),
            pltpu.VMEM((2, shard, 2 * span), F32),
            pltpu.VMEM((LANES, padded), F32),
            pltpu.VMEM((rows, 8, padded), F32),
            pltpu.VMEM((4, 8, padded), F32),
            pltpu.SemaphoreType.DMA((copies,)),
            pltpu.SemaphoreType.DMA((copies,)),
        ],
        compiler_params=pltpu.CompilerParams(
            collective_id=0, has_side_effects=True, vmem_limit_bytes=60 * 1024 * 1024
        ),
    )(
        latents.reshape(channels, cells),
        grad_output.reshape(channels, cells),
        norm_gains,
        norm_biases,
        time_shift,
        jnp.transpose(conv_first, (1, 0, 2)),
        jnp.transpose(conv_second, (1, 0, 2)),
        jnp.asarray(pool),
        jnp.asarray(np.ascontiguousarray(pool.T)),
    )
    return (
        out.reshape(latents.shape),
        gin.reshape(latents.shape),
        small[0:1, :channels],
        jnp.transpose(dw1, (1, 0, 2)),
        jnp.transpose(dw2, (1, 0, 2)),
        small[1:5, :channels],
    )


def solution(mesh):
    placed = (
        P(("groups", "zero"), None, "rows", None),
        P(("groups", "zero"), None),
        P("zero", None, None),
        P("zero", None, None),
        P(),
        P(),
        P(("groups", "zero"), None, "rows", None),
    )
    return jax.shard_map(
        local,
        mesh=mesh,
        in_specs=placed,
        out_specs=(
            P(("groups", "zero"), None, "rows", None),
            P(("groups", "zero"), None, "rows", None),
            P(("groups", "zero"), None),
            P(("groups", "zero"), None, None),
            P(("groups", "zero"), None, None),
            P("groups", None),
        ),
        check_vma=False,
    )
```
